32 devices in a mesh: grp: 2 (over y), row: 8 (over z, x), col: 2 (over core).
Axes of the slice: x: 2, y: 2, z: 4, core: 2. Of those that a mesh axis runs over, the one named last changes fastest.
Arguments:
- queries: bfloat16 [2048, 1536], P(('grp', 'row', 'col')), parts along dimension 0, may hold values from -24 to 24
- key_rows: bfloat16 [2048, 1536], P(('grp', 'row', 'col')), parts along dimension 0, may hold values from -8 to 8
- value_rows: bfloat16 [2048, 1536], P(('grp', 'row', 'col')), parts along dimension 0, may hold values from -6 to 6
- latent: float32 [2048, 128], P(('grp', 'row', 'col')), parts along dimension 0, may hold values from -6 to 6
- out_proj: bfloat16 [1536, 128], replicated, may hold values from -0.625 to 0.625
- tile_owner: int32 [512, 1], P(('grp', 'row', 'col')), parts along dimension 0, may hold values from 0 to 7; in each aligned block of 16 rows (0 to 15, 16 to 31, ...) at most 4 rows name the same one
- tile_count: int32 [512], P(('grp', 'row', 'col')), parts along dimension 0, may hold values from 3 to 4
- window_reach: int32 [2, 3], replicated, may hold values from 0 to 3
- refine_query: bfloat16 [128, 128], replicated, may hold values from -0.5 to 0.5
- refine_key: bfloat16 [128, 128], replicated, may hold values from -0.5 to 0.5
- refine_value: bfloat16 [128, 128], replicated, may hold values from -0.5 to 0.5
- refine_out: bfloat16 [128, 128], replicated, may hold values from -0.5 to 0.5
Outputs:
- updated: float32 [2048, 128], P(('grp', 'row', 'col')), parts along dimension 0
- refined: float32 [2048, 128], P(('grp', 'row', 'col')), parts along dimension 0
The draws below stay inside these ranges and needn't reach their ends.
There are 2 independent parts, one for each index of `grp`. The reference program is written for one: setup_inputs(seed, part) draws one part's arguments, and reference() takes and returns one part's arrays. A program takes and returns all parts, laid end to end along the dimension named above; an argument that names none is the same for every part. Nothing has to cross between parts.
Inputs may be any that keep to these rules, and one draw needn't show every extreme that they name: `tile_owner`: among the 16 tiles of one device no owner is named by more than 4 tiles, and some device reaches 4 for some owner.
All inputs are finite; a program needn't handle non-finite values.
Results may differ from the reference program's by a relative error of at most 0.024.
Values may be sent and summed in bfloat16 or wider, within the bound.
A program may use at most 128 MiB of HBM per device.

```python
import math
import jax
import jax.numpy as jnp
import numpy as np
from jax import lax

HEAD = 128
HEADS = 12
LAT = 128
RHEADS = 2
RHEAD = 64
TILE = 4
GW = 64
GH = 64
TOK_DEV = 64
TOKENS = 1024
TILES_DEV = 16
NTILES = 256
CAP = 4
N_ROW = 8
N_COL = 2


def base_keys(key):
    return jnp.clip(jax.random.normal(jax.random.fold_in(key, 11), (TOKENS, HEADS * HEAD), jnp.float32), -4.0, 4.0)


def draw_key_rows(key, part):
    rows = base_keys(key)
    return rows.astype(jnp.bfloat16)


def draw_queries(key, part):
    rows = jnp.clip(2.0 * jax.random.normal(jax.random.fold_in(key, 23), (TOKENS, HEADS * HEAD), jnp.float32), -8.0, 8.0)
    return rows.astype(jnp.bfloat16)


def set_ends(values, own_key, smallest, high):
    dims = values.shape
    spot = [jax.random.randint(jax.random.fold_in(own_key, axis), (), 0, dims[axis]) for axis in range(len(dims))]
    values = values.at[tuple(spot)].set(smallest)
    longest = dims.index(max(dims))
    spot[longest] = (spot[longest] + 1) % dims[longest]
    return values.at[tuple(spot)].set(high)


def levels(own_key, dims, cuts, least, high):
    def one(dim, blocks):
        steps = jax.random.uniform(jax.random.fold_in(jax.random.fold_in(own_key, 6), dim), (blocks,), jnp.float32, least / len(cuts), high / len(cuts))
        return jnp.repeat(jnp.exp(steps), dims[dim] // blocks).reshape((-1,) + (1,) * (len(dims) - dim - 1))

    gain = one(*cuts[0])
    for cut in cuts[1:]:
        gain = gain * one(*cut)
    return gain


def shared_out(rng, own, number, rows, amount, top, limit, slope):
    sequence = jax.random.permutation(rng, amount)
    packed, common = load_shares(amount, rows * top, limit, slope, True), load_shares(amount, rows * top, limit, slope, False)
    places = jnp.arange(amount)

    def named(tallies, turn):
        used = int((tallies > 0).sum())
        fixed = max(1, used // 4)
        passed = fixed + (places - fixed + turn * (used - fixed)) % max(1, amount - fixed)
        return jnp.zeros((amount,), jnp.int32).at[sequence[jnp.where(places < fixed, places, passed)]].set(jnp.asarray(tallies, jnp.int32))

    tallies = jnp.where(number % 4 == 0, named(packed, number // 4), named(common, number - number // 4 - 1))
    mixed = jax.random.permutation(jax.random.fold_in(own, 3), amount)
    giver, taker = mixed[0:amount // 2 * 2:2], mixed[1:amount // 2 * 2:2]
    slack = jnp.minimum(tallies[giver] - 1, limit - tallies[taker]) // 2
    slack = jnp.where((giver == sequence[0]) | (taker == sequence[0]) | (tallies[taker] == 0), 0, jnp.maximum(slack, 0))
    passed = jax.random.randint(jax.random.fold_in(own, 4), (amount // 2,), 0, 1 << 20) % (slack + 1)
    tallies = tallies.at[giver].add(-passed).at[taker].add(passed)
    labels = jnp.searchsorted(jnp.cumsum(tallies), jnp.arange(rows * top), side="right").astype(jnp.int32)
    table = labels.reshape(top, rows).T
    table = table[jax.random.permutation(jax.random.fold_in(own, 1), rows)]
    turn = jax.random.randint(jax.random.fold_in(own, 2), (rows, 1), 0, top)
    return jnp.take_along_axis(table, (jnp.arange(top)[None, :] + turn) % top, axis=1)


def load_shares(count, total, limit, slope, full):
    portions = [(1 << 20) // math.isqrt(grade ** slope) + 1 for grade in range(1, count + 1)]
    largest = limit if full else min(limit, max(-(-total // count), total * portions[0] // sum(portions)))
    least = 1 if total - largest >= count - 1 else 0
    counts, surplus = [largest] + [least] * (count - 1), total - largest - least * (count - 1)
    while surplus > 0:
        movable = [i for i in range(1, count) if counts[i] < largest] or [i for i in range(1, count) if counts[i] < limit]
        mass, budget = sum([portions[i] for i in movable]), surplus
        for i in movable:
            extra = min(limit - counts[i], max(1, budget * portions[i] // mass), surplus)
            counts[i] = counts[i] + extra
            surplus = surplus - extra
    return np.array(counts)


def centred(key, dims, width, reach, cuts=(), kind=jnp.bfloat16):
    entries = width * jax.random.normal(key, dims, jnp.float32)
    if cuts:
        entries = entries * levels(key, dims, cuts, -0.22, 0.18)
    return jnp.clip(entries, -reach, reach).astype(kind)


def setup_inputs(seed: int = 0, part: int = 0) -> dict:
    key_list = jax.random.split(jax.random.key(seed), 13)
    own_keys = jax.random.split(jax.random.fold_in(key_list[12], part), 13)
    queries = draw_queries(jax.random.fold_in(jax.random.fold_in(key_list[12], part), 71), part)
    key_rows = draw_key_rows(jax.random.fold_in(jax.random.fold_in(key_list[12], part), 71), part)
    value_rows = centred(own_keys[2], (TOKENS, HEADS * HEAD), 1.0, 6.0, ((0, 16),))
    latent = centred(own_keys[3], (TOKENS, LAT), 1.0, 6.0, ((0, 16),), jnp.float32)
    out_proj = centred(key_list[4], (HEADS * HEAD, LAT), (HEADS * 8) ** -0.5, 0.625)
    tile_owner_keys = jax.random.split(jax.random.fold_in(own_keys[5], 1), NTILES // TILES_DEV)
    tile_owner_turns = jax.random.permutation(jax.random.fold_in(own_keys[5], 3), NTILES // TILES_DEV)
    tile_owner = jax.vmap(lambda own, number: shared_out(jax.random.fold_in(own_keys[5], 2), own, number, TILES_DEV, N_ROW, 1, CAP, 2))(tile_owner_keys, tile_owner_turns).reshape((NTILES, 1))
    tile_count = set_ends(jax.random.randint(own_keys[6], (NTILES,), TILE - TILE // 4, TILE + 1), jax.random.fold_in(own_keys[6], 1), TILE - TILE // 4, TILE).astype(jnp.int32)
    window_reach = set_ends(jax.random.randint(key_list[7], (RHEADS, 3), 0, 4), jax.random.fold_in(key_list[7], 1), 0, 3).astype(jnp.int32)
    refine_query = centred(key_list[8], (LAT, LAT), LAT ** -0.5, 0.5)
    refine_key = centred(key_list[9], (LAT, LAT), LAT ** -0.5, 0.5)
    refine_value = centred(key_list[10], (LAT, LAT), LAT ** -0.5, 0.5)
    refine_out = centred(key_list[11], (LAT, LAT), LAT ** -0.5, 0.5)
    return {"queries": queries, "key_rows": key_rows, "value_rows": value_rows, "latent": latent, "out_proj": out_proj, "tile_owner": tile_owner, "tile_count": tile_count, "window_reach": window_reach, "refine_query": refine_query, "refine_key": refine_key, "refine_value": refine_value, "refine_out": refine_out}


def full_attention(queries, key_rows, value_rows):
    scale = 1.0 / math.sqrt(HEAD)
    block = math.gcd(TOKENS, 512)
    joined = []
    for head_pos in range(HEADS):
        lower = head_pos * HEAD
        key_head = key_rows[:, lower:lower + HEAD]
        value_head = value_rows[:, lower:lower + HEAD]
        query_blocks = queries[:, lower:lower + HEAD].reshape(TOKENS // block, block, HEAD)

        def one_block(query_block):
            scores = jnp.dot(query_block, key_head.T, preferred_element_type=jnp.float32) * scale
            largest = lax.optimization_barrier(jnp.max(scores, axis=1, keepdims=True))
            weights = jnp.exp(scores - largest)
            totals = lax.optimization_barrier(jnp.sum(weights, axis=1, keepdims=True))
            mixed = jnp.dot(weights.astype(jnp.bfloat16), value_head, preferred_element_type=jnp.float32)
            return (mixed / totals).astype(jnp.bfloat16)
        joined.append(lax.map(one_block, query_blocks).reshape(TOKENS, HEAD))
    return jnp.concatenate(joined, axis=1)

def refiner(updated, tile_owner, tile_count, window_reach, refine_query, refine_key, refine_value, refine_out):
    positions = jnp.arange(TOKENS, dtype=jnp.int32)
    tile_of = positions // TILE
    owners = tile_owner[:, 0][tile_of]
    groups = owners * N_COL + positions // TOK_DEV % N_COL
    live = positions % TILE < tile_count[tile_of]
    frames = positions // (GH * GW)
    heights = positions // GW % GH
    widths = positions % GW
    refine_in = updated.astype(jnp.bfloat16)
    rquery = jnp.dot(refine_in, refine_query, preferred_element_type=jnp.float32).astype(jnp.bfloat16)
    rkey = jnp.dot(refine_in, refine_key, preferred_element_type=jnp.float32).astype(jnp.bfloat16)
    rvalue = jnp.dot(refine_in, refine_value, preferred_element_type=jnp.float32).astype(jnp.bfloat16)
    scale = 1.0 / math.sqrt(RHEAD)
    block = math.gcd(TOKENS, 512)
    count = TOKENS // block
    joined = []
    for head_pos in range(RHEADS):
        lower = head_pos * RHEAD
        key_head = rkey[:, lower:lower + RHEAD]
        value_head = rvalue[:, lower:lower + RHEAD]

        def one_block(items):
            query_block, group_block, frame_block, height_block, width_block = items
            scores = jnp.dot(query_block, key_head.T, preferred_element_type=jnp.float32) * scale
            allowed = (group_block[:, None] == groups[None, :]) & live[None, :]
            allowed = allowed & (jnp.abs(frame_block[:, None] - frames[None, :]) <= window_reach[head_pos, 0])
            allowed = allowed & (jnp.abs(height_block[:, None] - heights[None, :]) <= window_reach[head_pos, 1])
            allowed = allowed & (jnp.abs(width_block[:, None] - widths[None, :]) <= window_reach[head_pos, 2])
            scores = jnp.where(allowed, scores, -1e+30)
            largest = lax.optimization_barrier(jnp.max(scores, axis=1, keepdims=True))
            weights = jnp.exp(scores - largest)
            totals = lax.optimization_barrier(jnp.sum(weights, axis=1, keepdims=True))
            mixed = jnp.dot(weights.astype(jnp.bfloat16), value_head, preferred_element_type=jnp.float32)
            return (mixed / totals).astype(jnp.bfloat16)
        items = (rquery[:, lower:lower + RHEAD].reshape(count, block, RHEAD), groups.reshape(count, block), frames.reshape(count, block), heights.reshape(count, block), widths.reshape(count, block))
        joined.append(lax.map(one_block, items).reshape(TOKENS, RHEAD))
    refine_heads = jnp.concatenate(joined, axis=1)
    delta = jnp.dot(refine_heads, refine_out, preferred_element_type=jnp.float32).astype(jnp.bfloat16)
    return updated + jnp.where(live[:, None], delta.astype(jnp.float32), jnp.float32(0.0))

def reference(queries, key_rows, value_rows, latent, out_proj, tile_owner, tile_count, window_reach, refine_query, refine_key, refine_value, refine_out):
    attended = full_attention(queries, key_rows, value_rows)
    velocity = jnp.dot(attended, out_proj, preferred_element_type=jnp.float32)
    updated = latent + 0.5 * velocity
    refined = refiner(updated, tile_owner, tile_count, window_reach, refine_query, refine_key, refine_value, refine_out)
    return (updated, refined)
```

```python
import functools
import math

import jax
import jax.numpy as jnp
import numpy as np
from jax import lax
from jax.experimental import pallas as pl
from jax.experimental.pallas import tpu as pltpu
from jax.sharding import PartitionSpec as P

HEAD = 128
LAT = 128
RHEADS = 2
TILE = 4
GW = 64
GH = 64
MAX_REACH = 3
MESH = pl.DeviceIdType.MESH
NEG = -1e30


def near_rows(rows, cols, tok):
    spots = {}
    for r in range(rows):
        for c in range(cols):
            p = (r * cols + c) * tok + np.arange(tok)
            spots[r, c] = np.unique(np.stack([p // (GH * GW), p // GW % GH], 1), axis=0)
    found = []
    for d in sorted(range(1 - rows, rows), key=abs):
        if d == 0:
            continue
        hit = False
        for r in range(max(0, -d), min(rows, rows - d)):
            for c in range(cols):
                gap = np.abs(spots[r, c][:, None] - spots[r + d, c][None])
                hit = hit or bool((gap.max(-1) <= MAX_REACH).any())
        if hit:
            found.append(d)
    return found


def kernel(
    dims, near,
    q_hbm, k_hbm, v_hbm, lat_hbm, wo_hbm, owner_hbm, count_hbm, reach_hbm,
    rq_hbm, rk_hbm, rv_hbm, ro_hbm,
    upd_ref, ref_ref,
    qb, kb, vb, wo, lat, rw, ro, acc, part_out, part_in, nb, code, bias,
    owner_ref, count_ref, reach_ref,
    z_send, z_recv, s_send, s_recv, c_send, c_recv, p_send, p_recv,
    n_send, n_recv, m_send, m_recv, own_sem, w_sem, i_sem,
):
    G, S, C, hg, T = dims
    R = G * S
    grp = lax.axis_index("grp")
    row = lax.axis_index("row")
    col = lax.axis_index("col")
    g = row // S
    s = row % S
    n_near = len(near)
    tiles = T // TILE

    def head_cols(group, h):
        return pl.ds(pl.multiple_of((group * hg + h) * HEAD, HEAD), HEAD)

    arrays = ((q_hbm, qb), (k_hbm, kb), (v_hbm, vb))

    def slot(a, h, group):
        return qb.at[h, group] if a == 0 else arrays[a][1].at[h, s, col, group]

    own = [
        [
            pltpu.make_async_copy(
                arrays[a][0].at[:, head_cols(g, h)], slot(a, h, g), own_sem.at[h, a]
            )
            for a in range(3)
        ]
        for h in range(hg)
    ]
    depth = hg * HEAD
    weights = [
        pltpu.make_async_copy(
            wo_hbm.at[pl.ds(pl.multiple_of(g * depth, depth), depth)], wo, w_sem.at[0]
        ),
        pltpu.make_async_copy(lat_hbm, lat, w_sem.at[1]),
        pltpu.make_async_copy(rq_hbm, rw.at[0], w_sem.at[2]),
        pltpu.make_async_copy(rk_hbm, rw.at[1], w_sem.at[3]),
        pltpu.make_async_copy(rv_hbm, rw.at[2], w_sem.at[4]),
        pltpu.make_async_copy(ro_hbm, ro, w_sem.at[5]),
    ]

    tables = [
        pltpu.make_async_copy(owner_hbm, owner_ref, i_sem.at[0]),
        pltpu.make_async_copy(count_hbm, count_ref, i_sem.at[1]),
        pltpu.make_async_copy(reach_hbm, reach_ref, i_sem.at[2]),
    ]

    barrier = pltpu.get_barrier_semaphore()
    greeted = (
        [(lax.rem(g + d, G) * S + s, col) for d in range(1, G)]
        + [(g * S + lax.rem(s + d, S), col) for d in range(1, S)]
        + [(row, lax.rem(col + d, C)) for d in range(1, C)]
    )
    for r2, c2 in greeted:
        pl.semaphore_signal(barrier, inc=1, device_id=(grp, r2, c2), device_id_type=MESH)

    for d in near:
        @pl.when((row + d >= 0) & (row + d < R))
        def _():
            pl.semaphore_signal(
                barrier, inc=1, device_id=(grp, row + d, col), device_id_type=MESH
            )

    for t in tables:
        t.start()
    for h in range(hg):
        for a in range(3):
            own[h][a].start()
    for w in weights:
        w.start()
    for t in tables:
        t.wait()

    lane = lax.broadcasted_iota(jnp.int32, (8, 128), 1)
    sub = lax.broadcasted_iota(jnp.int32, (T, 1), 0)
    code_row = jnp.full((8, 128), -1, jnp.int32)
    owner_col = jnp.zeros((T, 1), jnp.int32)
    live_col = jnp.zeros((T, 1), jnp.int32)
    for t in range(tiles):
        own_t, cnt_t = owner_ref[t], count_ref[t]
        code_row = jnp.where(
            (lane // TILE == t) & (lane % TILE < cnt_t) & (lane < T), own_t, code_row
        )
        owner_col = jnp.where(sub // TILE == t, own_t, owner_col)
        live_col = jnp.where((sub // TILE == t) & (sub % TILE < cnt_t), 1, live_col)
    code[0] = code_row.astype(jnp.float32)

    def near_ok(d):
        return (row - d >= 0) & (row - d < R)

    def goes(d):
        return (row + d >= 0) & (row + d < R)

    for i, d in enumerate(near):
        @pl.when(jnp.logical_not(near_ok(d)))
        def _():
            nb[i + 1] = jnp.zeros((T, LAT), jnp.bfloat16)
            code[i + 1] = jnp.full((8, 128), -1.0, jnp.float32)

    pl.semaphore_wait(
        barrier, len(greeted) + sum([near_ok(d).astype(jnp.int32) for d in near])
    )

    def z_copy(h, a, d):
        to = lax.rem(g + d, G)
        return pltpu.make_async_remote_copy(
            src_ref=arrays[a][0].at[:, head_cols(to, h)],
            dst_ref=slot(a, h, g),
            send_sem=z_send.at[h, a, d - 1],
            recv_sem=z_recv.at[h, a, d - 1],
            device_id=(grp, to * S + s, col),
            device_id_type=MESH,
        )

    z_copies = {}
    for h, a in [(h, a) for a in (1, 2, 0) for h in range(hg)]:
        for d in list(range(2, G)) + [1]:
            z_copies[h, a, d] = z_copy(h, a, d)
            z_copies[h, a, d].start()

    def m_copy(i, d):
        return pltpu.make_async_remote_copy(
            src_ref=code.at[0],
            dst_ref=code.at[i + 1],
            send_sem=m_send.at[i],
            recv_sem=m_recv.at[i],
            device_id=(grp, row + d, col),
            device_id_type=MESH,
        )

    for i, d in enumerate(near):
        @pl.when(goes(d))
        def _():
            m_copy(i, d).start()

    s_copies, c_copies = {}, {}

    def c_forward(h, a, j):
        buf = arrays[a][1]
        src = lax.rem(s - j + S, S)
        for d in range(1, C):
            c_copies[h, a, j, d] = pltpu.make_async_remote_copy(
                src_ref=buf.at[h, src, col],
                dst_ref=buf.at[h, src, col],
                send_sem=c_send.at[h, a - 1, j, d - 1],
                recv_sem=c_recv.at[h, a - 1, j, d - 1],
                device_id=(grp, row, lax.rem(col + d, C)),
                device_id_type=MESH,
            )
            c_copies[h, a, j, d].start()

    def s_forward(h, a, e):
        buf = arrays[a][1]
        block = buf.at[h, s, col, lax.rem(g - e + G, G)]
        for d in range(1, S):
            s_copies[h, a, e, d] = pltpu.make_async_remote_copy(
                src_ref=block,
                dst_ref=block,
                send_sem=s_send.at[h, a - 1, e, d - 1],
                recv_sem=s_recv.at[h, a - 1, e, d - 1],
                device_id=(grp, g * S + lax.rem(s + d, S), col),
                device_id_type=MESH,
            )
            s_copies[h, a, e, d].start()

    def spread(h, kinds=(1, 2)):
        for a in kinds:
            for e in range(1, G):
                z_copies[h, a, e].wait_recv()
                s_forward(h, a, e)
            c_forward(h, a, 0)

    def pass_on(h, kinds=(1, 2)):
        for a in kinds:
            for d in range(1, S):
                for e in range(G):
                    s_copies[h, a, e, d].wait_recv()
                c_forward(h, a, d)

    keys = S * C * G * T
    fold = math.log2(math.e) / math.sqrt(HEAD)

    def soften(h):
        query = qb[h].reshape(G * T, HEAD)
        key = kb[h].reshape(keys, HEAD)
        scores = lax.dot_general(
            query, key, (((1,), (1,)), ((), ())), preferred_element_type=jnp.float32
        )
        largest = jnp.max(scores, axis=1, keepdims=True)
        terms = jnp.exp2((scores - largest) * fold)
        return terms.astype(jnp.bfloat16), jnp.sum(terms, axis=1, keepdims=True)

    def blend(h, terms, total):
        value = vb[h].reshape(keys, HEAD)
        mixed = jnp.dot(terms, value, preferred_element_type=jnp.float32)
        attended = (mixed / total).astype(jnp.bfloat16)
        share = jnp.dot(
            attended, wo[h * HEAD : (h + 1) * HEAD], preferred_element_type=jnp.float32
        ).reshape(G, T, LAT)
        return share if h == 0 else acc[...] + share

    def c_arrive(h, a):
        for j in range(S):
            for d in range(1, C):
                c_copies[h, a, j, d].wait_recv()

    def weigh(h):
        own[h][0].wait()
        for d in range(1, G):
            z_copies[h, 0, d].wait_recv()
        c_arrive(h, 1)
        return soften(h)

    for h in range(hg):
        for a in (1, 2):
            own[h][a].wait()
            s_forward(h, a, 0)
    for w in weights:
        w.wait()
    for a in (1, 2):
        for h in range(hg):
            spread(h, (a,))
    for h in range(hg):
        pass_on(h, (1,))
    for h in range(1, hg):
        if h == 1:
            for i, d in enumerate(near):
                @pl.when(near_ok(d))
                def _():
                    m_copy(i, d).wait_recv()
            codes = jnp.concatenate([code[i, 0:1, 0:T] for i in range(n_near + 1)], axis=1)
            spots = jnp.concatenate(
                [
                    ((row - d) * C + col) * T + lax.broadcasted_iota(jnp.int32, (1, T), 1)
                    for d in [0] + near
                ],
                axis=1,
            )
            mine = (row * C + col) * T + sub
            same = codes == owner_col.astype(jnp.float32)
            gap_f = jnp.abs(mine // (GH * GW) - spots // (GH * GW))
            gap_h = jnp.abs(mine // GW % GH - spots // GW % GH)
            gap_w = jnp.abs(mine % GW - spots % GW)
            for j in range(RHEADS):
                ok = (
                    same
                    & (gap_f <= reach_ref[j, 0])
                    & (gap_h <= reach_ref[j, 1])
                    & (gap_w <= reach_ref[j, 2])
                )
                bias[j * T : (j + 1) * T] = jnp.where(ok, 0.0, NEG)
    last = hg - 1
    weighed = []
    for h in range(last):
        pass_on(h, (2,))
        weighed.append(weigh(h))
    pass_on(last, (2,))
    for h in range(last):
        c_arrive(h, 2)
        acc[...] = blend(h, *weighed[h])
    weighed.append(weigh(last))
    c_arrive(last, 2)
    share = blend(last, *weighed[last])
    part_out[...] = share.astype(jnp.bfloat16)
    p_copies = {}
    for d in range(1, G):
        to = lax.rem(g + d, G)
        p_copies[d] = pltpu.make_async_remote_copy(
            src_ref=part_out.at[to],
            dst_ref=part_in.at[d - 1],
            send_sem=p_send.at[d - 1],
            recv_sem=p_recv.at[d - 1],
            device_id=(grp, to * S + s, col),
            device_id_type=MESH,
        )
        p_copies[d].start()
    acc[...] = share
    velocity = acc[g]
    for d in range(1, G):
        p_copies[d].wait_recv()
        velocity = velocity + part_in[d - 1].astype(jnp.float32)
    updated = lat[...] + 0.5 * velocity
    fine = updated.astype(jnp.bfloat16)
    nb[0] = fine

    def n_copy(i, d):
        return pltpu.make_async_remote_copy(
            src_ref=nb.at[0],
            dst_ref=nb.at[i + 1],
            send_sem=n_send.at[i],
            recv_sem=n_recv.at[i],
            device_id=(grp, row + d, col),
            device_id_type=MESH,
        )

    for i, d in enumerate(near):
        @pl.when(goes(d))
        def _():
            n_copy(i, d).start()
    upd_ref[...] = 0.5 * velocity
    rquery = jnp.dot(fine, rw[0], preferred_element_type=jnp.float32).astype(jnp.bfloat16)
    rhead = LAT // RHEADS
    part_of = lax.broadcasted_iota(jnp.int32, (T, LAT), 1) // rhead
    stacked = jnp.concatenate(
        [jnp.where(part_of == j, rquery, jnp.zeros_like(rquery)) for j in range(RHEADS)], axis=0
    )
    for i, d in enumerate(near):
        @pl.when(near_ok(d))
        def _():
            n_copy(i, d).wait_recv()
    around = nb[...].reshape((n_near + 1) * T, LAT)
    rkey = jnp.dot(around, rw[1], preferred_element_type=jnp.float32).astype(jnp.bfloat16)
    rvalue = jnp.dot(around, rw[2], preferred_element_type=jnp.float32).astype(jnp.bfloat16)
    scores = lax.dot_general(
        stacked, rkey, (((1,), (1,)), ((), ())), preferred_element_type=jnp.float32
    )
    scores = scores * (1.0 / math.sqrt(rhead)) + bias[...]
    terms = jnp.exp(scores - jnp.max(scores, axis=1, keepdims=True))
    total = jnp.sum(terms, axis=1, keepdims=True)
    mixed = jnp.dot(terms.astype(jnp.bfloat16), rvalue, preferred_element_type=jnp.float32) / total
    joined = mixed[0:T]
    for j in range(1, RHEADS):
        joined = jnp.where(part_of == j, mixed[j * T : (j + 1) * T], joined)
    delta = jnp.dot(
        joined.astype(jnp.bfloat16), ro[...], preferred_element_type=jnp.float32
    ).astype(jnp.bfloat16)
    ref_ref[...] = jnp.where(live_col > 0, delta.astype(jnp.float32), 0.0)

    for copies in (z_copies, s_copies, c_copies, p_copies):
        for copy in copies.values():
            copy.wait_send()
    for i, d in enumerate(near):
        @pl.when(goes(d))
        def _():
            m_copy(i, d).wait_send()
            n_copy(i, d).wait_send()


def per_device(
    queries, key_rows, value_rows, latent, out_proj, tile_owner, tile_count, window_reach,
    refine_query, refine_key, refine_value, refine_out,
):
    R, C = lax.axis_size("row"), lax.axis_size("col")
    T = queries.shape[0]
    heads = queries.shape[1] // HEAD
    G = math.gcd(heads, R)
    S = R // G
    hg = heads // G
    near = near_rows(R, C, T)
    n = len(near)
    any_spec = pl.BlockSpec(memory_space=pl.ANY)
    vmem = pl.BlockSpec(memory_space=pltpu.VMEM)
    dma = pltpu.SemaphoreType.DMA
    bf16, f32 = jnp.bfloat16, jnp.float32
    half, delta = pl.pallas_call(
        functools.partial(kernel, (G, S, C, hg, T), near),
        out_shape=(
            pltpu.VMEM((T, LAT), f32),
            pltpu.VMEM((T, LAT), f32),
        ),
        in_specs=[any_spec] * 12,
        out_specs=(vmem, vmem),
        scratch_shapes=[
            pltpu.VMEM((hg, G, T, HEAD), bf16),
            pltpu.VMEM((hg, S, C, G, T, HEAD), bf16),
            pltpu.VMEM((hg, S, C, G, T, HEAD), bf16),
            pltpu.VMEM((hg * HEAD, LAT), bf16),
            pltpu.VMEM((T, LAT), f32),
            pltpu.VMEM((3, LAT, LAT), bf16),
            pltpu.VMEM((LAT, LAT), bf16),
            pltpu.VMEM((G, T, LAT), f32),
            pltpu.VMEM((G, T, LAT), bf16),
            pltpu.VMEM((G - 1, T, LAT), bf16),
            pltpu.VMEM((n + 1, T, LAT), bf16),
            pltpu.VMEM((n + 1, 8, 128), f32),
            pltpu.VMEM((RHEADS * T, (n + 1) * T), f32),
            pltpu.SMEM((T // TILE,), jnp.int32),
            pltpu.SMEM((T // TILE,), jnp.int32),
            pltpu.SMEM((RHEADS, 3), jnp.int32),
            dma((hg, 3, G - 1)),
            dma((hg, 3, G - 1)),
            dma((hg, 2, G, max(S - 1, 1))),
            dma((hg, 2, G, max(S - 1, 1))),
            dma((hg, 2, S, max(C - 1, 1))),
            dma((hg, 2, S, max(C - 1, 1))),
            dma((G - 1,)),
            dma((G - 1,)),
            dma((n,)),
            dma((n,)),
            dma((n,)),
            dma((n,)),
            dma((hg, 3)),
            dma((6,)),
            dma((3,)),
        ],
        compiler_params=pltpu.CompilerParams(collective_id=0, has_side_effects=True),
    )(
        queries, key_rows, value_rows, latent, out_proj, tile_owner.reshape(-1), tile_count,
        window_reach, refine_query, refine_key, refine_value, refine_out,
    )
    updated = latent + half
    return updated, updated + delta


def solution(mesh):
    return jax.shard_map(
        per_device,
        mesh=mesh,
        in_specs=(
            P(("grp", "row", "col"), None),
            P(("grp", "row", "col"), None),
            P(("grp", "row", "col"), None),
            P(("grp", "row", "col"), None),
            P(),
            P(("grp", "row", "col"), None),
            P(("grp", "row", "col")),
            P(),
            P(),
            P(),
            P(),
            P(),
        ),
        out_specs=(P(("grp", "row", "col"), None), P(("grp", "row", "col"), None)),
        check_vma=False,
    )
```

```python
import functools
import math

import jax
import jax.numpy as jnp
import numpy as np
from jax import lax
from jax.experimental import pallas as pl
from jax.experimental.pallas import tpu as pltpu
from jax.sharding import PartitionSpec as P

HEAD = 128
LAT = 128
RHEADS = 2
TILE = 4
GW = 64
GH = 64
MAX_REACH = 3
MESH = pl.DeviceIdType.MESH
NEG = -1e30


def near_rows(rows, cols, tok):
    spots = {}
    for r in range(rows):
        for c in range(cols):
            p = (r * cols + c) * tok + np.arange(tok)
            spots[r, c] = np.unique(np.stack([p // (GH * GW), p // GW % GH], 1), axis=0)
    found = []
    for d in sorted(range(1 - rows, rows), key=abs):
        if d == 0:
            continue
        hit = False
        for r in range(max(0, -d), min(rows, rows - d)):
            for c in range(cols):
                gap = np.abs(spots[r, c][:, None] - spots[r + d, c][None])
                hit = hit or bool((gap.max(-1) <= MAX_REACH).any())
        if hit:
            found.append(d)
    return found


def kernel(
    dims, near,
    q_hbm, k_hbm, v_hbm, lat_hbm, wo_hbm, owner_hbm, count_hbm, reach_hbm,
    rq_hbm, rk_hbm, rv_hbm, ro_hbm,
    upd_ref, ref_ref,
    qb, kb, vb, wo, lat, rw, ro, acc, part_out, part_in, nb, code, bias,
    owner_ref, count_ref, reach_ref,
    z_send, z_recv, s_send, s_recv, c_send, c_recv, p_send, p_recv,
    n_send, n_recv, m_send, m_recv, own_sem, w_sem, i_sem,
):
    G, S, C, hg, T = dims
    R = G * S
    grp = lax.axis_index("grp")
    row = lax.axis_index("row")
    col = lax.axis_index("col")
    g = row // S
    s = row % S
    n_near = len(near)
    tiles = T // TILE

    def head_cols(group, h):
        return pl.ds(pl.multiple_of((group * hg + h) * HEAD, HEAD), HEAD)

    arrays = ((q_hbm, qb), (k_hbm, kb), (v_hbm, vb))

    def slot(a, h, group):
        return qb.at[h, group] if a == 0 else arrays[a][1].at[h, s, col, group]

    own = [
        [
            pltpu.make_async_copy(
                arrays[a][0].at[:, head_cols(g, h)], slot(a, h, g), own_sem.at[h, a]
            )
            for a in range(3)
        ]
        for h in range(hg)
    ]
    depth = hg * HEAD
    weights = [
        pltpu.make_async_copy(
            wo_hbm.at[pl.ds(pl.multiple_of(g * depth, depth), depth)], wo, w_sem.at[0]
        ),
        pltpu.make_async_copy(lat_hbm, lat, w_sem.at[1]),
        pltpu.make_async_copy(rq_hbm, rw.at[0], w_sem.at[2]),
        pltpu.make_async_copy(rk_hbm, rw.at[1], w_sem.at[3]),
        pltpu.make_async_copy(rv_hbm, rw.at[2], w_sem.at[4]),
        pltpu.make_async_copy(ro_hbm, ro, w_sem.at[5]),
    ]

    tables = [
        pltpu.make_async_copy(owner_hbm, owner_ref, i_sem.at[0]),
        pltpu.make_async_copy(count_hbm, count_ref, i_sem.at[1]),
        pltpu.make_async_copy(reach_hbm, reach_ref, i_sem.at[2]),
    ]

    barrier = pltpu.get_barrier_semaphore()
    greeted = (
        [(lax.rem(g + d, G) * S + s, col) for d in range(1, G)]
        + [(g * S + lax.rem(s + d, S), col) for d in range(1, S)]
        + [(row, lax.rem(col + d, C)) for d in range(1, C)]
    )
    for r2, c2 in greeted:
        pl.semaphore_signal(barrier, inc=1, device_id=(grp, r2, c2), device_id_type=MESH)

    for d in near:
        @pl.when((row + d >= 0) & (row + d < R))
        def _():
            pl.semaphore_signal(
                barrier, inc=1, device_id=(grp, row + d, col), device_id_type=MESH
            )

    for t in tables:
        t.start()
    for h in range(hg):
        for a in range(3):
            own[h][a].start()
    for w in weights:
        w.start()
    for t in tables:
        t.wait()

    lane = lax.broadcasted_iota(jnp.int32, (8, 128), 1)
    sub = lax.broadcasted_iota(jnp.int32, (T, 1), 0)
    code_row = jnp.full((8, 128), -1, jnp.int32)
    owner_col = jnp.zeros((T, 1), jnp.int32)
    live_col = jnp.zeros((T, 1), jnp.int32)
    for t in range(tiles):
        own_t, cnt_t = owner_ref[t], count_ref[t]
        code_row = jnp.where(
            (lane // TILE == t) & (lane % TILE < cnt_t) & (lane < T), own_t, code_row
        )
        owner_col = jnp.where(sub // TILE == t, own_t, owner_col)
        live_col = jnp.where((sub // TILE == t) & (sub % TILE < cnt_t), 1, live_col)
    code[0] = code_row.astype(jnp.float32)

    def near_ok(d):
        return (row - d >= 0) & (row - d < R)

    def goes(d):
        return (row + d >= 0) & (row + d < R)

    for i, d in enumerate(near):
        @pl.when(jnp.logical_not(near_ok(d)))
        def _():
            nb[i + 1] = jnp.zeros((T, LAT), jnp.bfloat16)
            code[i + 1] = jnp.full((8, 128), -1.0, jnp.float32)

    pl.semaphore_wait(
        barrier, len(greeted) + sum([near_ok(d).astype(jnp.int32) for d in near])
    )

    def far(k):
        down = jnp.where(G - 1 - k > g, G - 1 - k, G - 2 - k)
        return jnp.where(2 * g < G, down, jnp.where(k < g, k, k + 1))

    def close(k):
        return far(G - 2 - k)

    def z_copy(h, a, to):
        return pltpu.make_async_remote_copy(
            src_ref=arrays[a][0].at[:, head_cols(to, h)],
            dst_ref=slot(a, h, g),
            send_sem=z_send.at[h, a, to],
            recv_sem=z_recv.at[h, a, g],
            device_id=(grp, to * S + s, col),
            device_id_type=MESH,
        )

    z_copies = {}
    def z_start(kinds):
        for h, a in [(h, a) for a in kinds for h in range(hg)]:
            for k in range(G - 1):
                z_copies[h, a, k] = z_copy(h, a, far(k))
                z_copies[h, a, k].start()

    def z_arrived(h, a, frm):
        pltpu.make_async_remote_copy(
            src_ref=slot(a, h, frm),
            dst_ref=slot(a, h, frm),
            send_sem=z_send.at[h, a, frm],
            recv_sem=z_recv.at[h, a, frm],
            device_id=(grp, frm * S + s, col),
            device_id_type=MESH,
        ).wait_recv()

    z_start((1, 2))

    def m_copy(i, d):
        return pltpu.make_async_remote_copy(
            src_ref=code.at[0],
            dst_ref=code.at[i + 1],
            send_sem=m_send.at[i],
            recv_sem=m_recv.at[i],
            device_id=(grp, row + d, col),
            device_id_type=MESH,
        )

    for i, d in enumerate(near):
        @pl.when(goes(d))
        def _():
            m_copy(i, d).start()

    s_copies, c_copies = {}, {}

    def c_forward(h, a, j):
        buf = arrays[a][1]
        src = lax.rem(s - j + S, S)
        for d in range(1, C):
            c_copies[h, a, j, d] = pltpu.make_async_remote_copy(
                src_ref=buf.at[h, src, col],
                dst_ref=buf.at[h, src, col],
                send_sem=c_send.at[h, a - 1, j, d - 1],
                recv_sem=c_recv.at[h, a - 1, j, d - 1],
                device_id=(grp, row, lax.rem(col + d, C)),
                device_id_type=MESH,
            )
            c_copies[h, a, j, d].start()

    def s_forward(h, a, frm, e):
        buf = arrays[a][1]
        block = buf.at[h, s, col, frm]
        for d in range(1, S):
            s_copies[h, a, e, d] = pltpu.make_async_remote_copy(
                src_ref=block,
                dst_ref=block,
                send_sem=s_send.at[h, a - 1, frm, d - 1],
                recv_sem=s_recv.at[h, a - 1, frm, d - 1],
                device_id=(grp, g * S + lax.rem(s + d, S), col),
                device_id_type=MESH,
            )
            s_copies[h, a, e, d].start()

    def spread(h, kinds=(1, 2)):
        for a in kinds:
            for k in range(G - 1):
                z_arrived(h, a, close(k))
                s_forward(h, a, close(k), k + 1)
            c_forward(h, a, 0)

    def pass_on(h, kinds=(1, 2)):
        for a in kinds:
            for d in range(1, S):
                for e in range(G):
                    s_copies[h, a, e, d].wait_recv()
                c_forward(h, a, d)

    keys = S * C * G * T
    fold = math.log2(math.e) / math.sqrt(HEAD)

    def soften(h):
        query = qb[h].reshape(G * T, HEAD)
        key = kb[h].reshape(keys, HEAD)
        scores = lax.dot_general(
            query, key, (((1,), (1,)), ((), ())), preferred_element_type=jnp.float32
        )
        largest = jnp.max(scores, axis=1, keepdims=True)
        terms = jnp.exp2((scores - largest) * fold)
        return terms.astype(jnp.bfloat16), jnp.sum(terms, axis=1, keepdims=True)

    def blend(h, terms, total):
        value = vb[h].reshape(keys, HEAD)
        mixed = jnp.dot(terms, value, preferred_element_type=jnp.float32)
        attended = (mixed / total).astype(jnp.bfloat16)
        share = jnp.dot(
            attended, wo[h * HEAD : (h + 1) * HEAD], preferred_element_type=jnp.float32
        ).reshape(G, T, LAT)
        return share if h == 0 else acc[...] + share

    def c_arrive(h, a):
        for j in range(S):
            for d in range(1, C):
                c_copies[h, a, j, d].wait_recv()

    def weigh(h):
        own[h][0].wait()
        for k in range(G - 1):
            z_arrived(h, 0, close(k))
        c_arrive(h, 1)
        return soften(h)

    for h in range(hg):
        for a in (1, 2):
            own[h][a].wait()
            s_forward(h, a, g, 0)
    for w in weights:
        w.wait()
    for h in range(hg):
        spread(h, (1,))
    for h in range(hg):
        spread(h, (2,))
        if h == 1:
            z_start((0,))
    for h in range(hg):
        pass_on(h, (1,))
    for h in range(1, hg):
        if h == 1:
            for i, d in enumerate(near):
                @pl.when(near_ok(d))
                def _():
                    m_copy(i, d).wait_recv()
            codes = jnp.concatenate([code[i, 0:1, 0:T] for i in range(n_near + 1)], axis=1)
            spots = jnp.concatenate(
                [
                    ((row - d) * C + col) * T + lax.broadcasted_iota(jnp.int32, (1, T), 1)
                    for d in [0] + near
                ],
                axis=1,
            )
            mine = (row * C + col) * T + sub
            same = codes == owner_col.astype(jnp.float32)
            gap_f = jnp.abs(mine // (GH * GW) - spots // (GH * GW))
            gap_h = jnp.abs(mine // GW % GH - spots // GW % GH)
            gap_w = jnp.abs(mine % GW - spots % GW)
            for j in range(RHEADS):
                ok = (
                    same
                    & (gap_f <= reach_ref[j, 0])
                    & (gap_h <= reach_ref[j, 1])
                    & (gap_w <= reach_ref[j, 2])
                )
                bias[j * T : (j + 1) * T] = jnp.where(ok, 0.0, NEG)
    last = hg - 1
    weighed = []
    for h in range(last):
        pass_on(h, (2,))
        weighed.append(weigh(h))
    pass_on(last, (2,))
    for h in range(last):
        c_arrive(h, 2)
        acc[...] = blend(h, *weighed[h])
    weighed.append(weigh(last))
    c_arrive(last, 2)
    share = blend(last, *weighed[last])
    part_out[...] = share.astype(jnp.bfloat16)
    p_copies = {}
    for k in range(G - 1):
        to = far(k)
        p_copies[k] = pltpu.make_async_remote_copy(
            src_ref=part_out.at[to],
            dst_ref=part_in.at[g],
            send_sem=p_send.at[to],
            recv_sem=p_recv.at[g],
            device_id=(grp, to * S + s, col),
            device_id_type=MESH,
        )
        p_copies[k].start()
    acc[...] = share
    velocity = acc[g]
    for k in range(G - 1):
        frm = close(k)
        pltpu.make_async_remote_copy(
            src_ref=part_in.at[frm],
            dst_ref=part_in.at[frm],
            send_sem=p_send.at[frm],
            recv_sem=p_recv.at[frm],
            device_id=(grp, frm * S + s, col),
            device_id_type=MESH,
        ).wait_recv()
        velocity = velocity + part_in[frm].astype(jnp.float32)
    updated = lat[...] + 0.5 * velocity
    fine = updated.astype(jnp.bfloat16)
    nb[0] = fine

    def n_copy(i, d):
        return pltpu.make_async_remote_copy(
            src_ref=nb.at[0],
            dst_ref=nb.at[i + 1],
            send_sem=n_send.at[i],
            recv_sem=n_recv.at[i],
            device_id=(grp, row + d, col),
            device_id_type=MESH,
        )

    for i, d in enumerate(near):
        @pl.when(goes(d))
        def _():
            n_copy(i, d).start()
    upd_ref[...] = 0.5 * velocity
    rquery = jnp.dot(fine, rw[0], preferred_element_type=jnp.float32).astype(jnp.bfloat16)
    rhead = LAT // RHEADS
    part_of = lax.broadcasted_iota(jnp.int32, (T, LAT), 1) // rhead
    stacked = jnp.concatenate(
        [jnp.where(part_of == j, rquery, jnp.zeros_like(rquery)) for j in range(RHEADS)], axis=0
    )
    for i, d in enumerate(near):
        @pl.when(near_ok(d))
        def _():
            n_copy(i, d).wait_recv()
    around = nb[...].reshape((n_near + 1) * T, LAT)
    rkey = jnp.dot(around, rw[1], preferred_element_type=jnp.float32).astype(jnp.bfloat16)
    rvalue = jnp.dot(around, rw[2], preferred_element_type=jnp.float32).astype(jnp.bfloat16)
    scores = lax.dot_general(
        stacked, rkey, (((1,), (1,)), ((), ())), preferred_element_type=jnp.float32
    )
    scores = scores * (1.0 / math.sqrt(rhead)) + bias[...]
    terms = jnp.exp(scores - jnp.max(scores, axis=1, keepdims=True))
    total = jnp.sum(terms, axis=1, keepdims=True)
    mixed = jnp.dot(terms.astype(jnp.bfloat16), rvalue, preferred_element_type=jnp.float32) / total
    joined = mixed[0:T]
    for j in range(1, RHEADS):
        joined = jnp.where(part_of == j, mixed[j * T : (j + 1) * T], joined)
    delta = jnp.dot(
        joined.astype(jnp.bfloat16), ro[...], preferred_element_type=jnp.float32
    ).astype(jnp.bfloat16)
    ref_ref[...] = jnp.where(live_col > 0, delta.astype(jnp.float32), 0.0)

    for copies in (z_copies, s_copies, c_copies, p_copies):
        for copy in copies.values():
            copy.wait_send()
    for i, d in enumerate(near):
        @pl.when(goes(d))
        def _():
            m_copy(i, d).wait_send()
            n_copy(i, d).wait_send()


def per_device(
    queries, key_rows, value_rows, latent, out_proj, tile_owner, tile_count, window_reach,
    refine_query, refine_key, refine_value, refine_out,
):
    R, C = lax.axis_size("row"), lax.axis_size("col")
    T = queries.shape[0]
    heads = queries.shape[1] // HEAD
    G = math.gcd(heads, R)
    S = R // G
    hg = heads // G
    near = near_rows(R, C, T)
    n = len(near)
    any_spec = pl.BlockSpec(memory_space=pl.ANY)
    vmem = pl.BlockSpec(memory_space=pltpu.VMEM)
    dma = pltpu.SemaphoreType.DMA
    bf16, f32 = jnp.bfloat16, jnp.float32
    half, delta = pl.pallas_call(
        functools.partial(kernel, (G, S, C, hg, T), near),
        out_shape=(
            pltpu.VMEM((T, LAT), f32),
            pltpu.VMEM((T, LAT), f32),
        ),
        in_specs=[any_spec] * 12,
        out_specs=(vmem, vmem),
        scratch_shapes=[
            pltpu.VMEM((hg, G, T, HEAD), bf16),
            pltpu.VMEM((hg, S, C, G, T, HEAD), bf16),
            pltpu.VMEM((hg, S, C, G, T, HEAD), bf16),
            pltpu.VMEM((hg * HEAD, LAT), bf16),
            pltpu.VMEM((T, LAT), f32),
            pltpu.VMEM((3, LAT, LAT), bf16),
            pltpu.VMEM((LAT, LAT), bf16),
            pltpu.VMEM((G, T, LAT), f32),
            pltpu.VMEM((G, T, LAT), bf16),
            pltpu.VMEM((G, T, LAT), bf16),
            pltpu.VMEM((n + 1, T, LAT), bf16),
            pltpu.VMEM((n + 1, 8, 128), f32),
            pltpu.VMEM((RHEADS * T, (n + 1) * T), f32),
            pltpu.SMEM((T // TILE,), jnp.int32),
            pltpu.SMEM((T // TILE,), jnp.int32),
            pltpu.SMEM((RHEADS, 3), jnp.int32),
            dma((hg, 3, G)),
            dma((hg, 3, G)),
            dma((hg, 2, G, max(S - 1, 1))),
            dma((hg, 2, G, max(S - 1, 1))),
            dma((hg, 2, S, max(C - 1, 1))),
            dma((hg, 2, S, max(C - 1, 1))),
            dma((G,)),
            dma((G,)),
            dma((n,)),
            dma((n,)),
            dma((n,)),
            dma((n,)),
            dma((hg, 3)),
            dma((6,)),
            dma((3,)),
        ],
        compiler_params=pltpu.CompilerParams(collective_id=0, has_side_effects=True),
    )(
        queries, key_rows, value_rows, latent, out_proj, tile_owner.reshape(-1), tile_count,
        window_reach, refine_query, refine_key, refine_value, refine_out,
    )
    updated = latent + half
    return updated, updated + delta


def solution(mesh):
    return jax.shard_map(
        per_device,
        mesh=mesh,
        in_specs=(
            P(("grp", "row", "col"), None),
            P(("grp", "row", "col"), None),
            P(("grp", "row", "col"), None),
            P(("grp", "row", "col"), None),
            P(),
            P(("grp", "row", "col"), None),
            P(("grp", "row", "col")),
            P(),
            P(),
            P(),
            P(),
            P(),
        ),
        out_specs=(P(("grp", "row", "col"), None), P(("grp", "row", "col"), None)),
        check_vma=False,
    )
```

```python
import functools
import math

import jax
import jax.numpy as jnp
import numpy as np
from jax import lax
from jax.experimental import pallas as pl
from jax.experimental.pallas import tpu as pltpu
from jax.sharding import PartitionSpec as P

HEAD = 128
LAT = 128
RHEADS = 2
TILE = 4
GW = 64
GH = 64
MAX_REACH = 3
MESH = pl.DeviceIdType.MESH
NEG = -1e30


def near_rows(rows, cols, tok):
    spots = {}
    for r in range(rows):
        for c in range(cols):
            p = (r * cols + c) * tok + np.arange(tok)
            spots[r, c] = np.unique(np.stack([p // (GH * GW), p // GW % GH], 1), axis=0)
    found = []
    for d in sorted(range(1 - rows, rows), key=abs):
        if d == 0:
            continue
        hit = False
        for r in range(max(0, -d), min(rows, rows - d)):
            for c in range(cols):
                gap = np.abs(spots[r, c][:, None] - spots[r + d, c][None])
                hit = hit or bool((gap.max(-1) <= MAX_REACH).any())
        if hit:
            found.append(d)
    return found


def kernel(
    dims, near,
    q_hbm, k_hbm, v_hbm, lat_hbm, wo_hbm, owner_hbm, count_hbm, reach_hbm,
    rq_hbm, rk_hbm, rv_hbm, ro_hbm,
    upd_ref, ref_ref,
    qb, kb, vb, wo, lat, rw, ro, acc, part_out, part_in, nb, code, bias,
    owner_ref, count_ref, reach_ref,
    z_send, z_recv, s_send, s_recv, c_send, c_recv, p_send, p_recv,
    n_send, n_recv, m_send, m_recv, own_sem, w_sem, i_sem,
):
    G, S, C, hg, T = dims
    R = G * S
    grp = lax.axis_index("grp")
    row = lax.axis_index("row")
    col = lax.axis_index("col")
    g = row // S
    s = row % S
    n_near = len(near)
    tiles = T // TILE

    def head_cols(group, h):
        return pl.ds(pl.multiple_of((group * hg + h) * HEAD, HEAD), HEAD)

    arrays = ((q_hbm, qb), (k_hbm, kb), (v_hbm, vb))

    def slot(a, h, group):
        return qb.at[h, group] if a == 0 else arrays[a][1].at[h, s, col, group]

    own = [
        [
            pltpu.make_async_copy(
                arrays[a][0].at[:, head_cols(g, h)], slot(a, h, g), own_sem.at[h, a]
            )
            for a in range(3)
        ]
        for h in range(hg)
    ]
    depth = hg * HEAD
    weights = [
        pltpu.make_async_copy(
            wo_hbm.at[pl.ds(pl.multiple_of(g * depth, depth), depth)], wo, w_sem.at[0]
        ),
        pltpu.make_async_copy(lat_hbm, lat, w_sem.at[1]),
        pltpu.make_async_copy(rq_hbm, rw.at[0], w_sem.at[2]),
        pltpu.make_async_copy(rk_hbm, rw.at[1], w_sem.at[3]),
        pltpu.make_async_copy(rv_hbm, rw.at[2], w_sem.at[4]),
        pltpu.make_async_copy(ro_hbm, ro, w_sem.at[5]),
    ]

    tables = [
        pltpu.make_async_copy(owner_hbm, owner_ref, i_sem.at[0]),
        pltpu.make_async_copy(count_hbm, count_ref, i_sem.at[1]),
        pltpu.make_async_copy(reach_hbm, reach_ref, i_sem.at[2]),
    ]

    barrier = pltpu.get_barrier_semaphore()
    greeted = (
        [(lax.rem(g + d, G) * S + s, col) for d in range(1, G)]
        + [(g * S + lax.rem(s + d, S), col) for d in range(1, S)]
        + [(row, lax.rem(col + d, C)) for d in range(1, C)]
    )
    for r2, c2 in greeted:
        pl.semaphore_signal(barrier, inc=1, device_id=(grp, r2, c2), device_id_type=MESH)

    for d in near:
        @pl.when((row + d >= 0) & (row + d < R))
        def _():
            pl.semaphore_signal(
                barrier, inc=1, device_id=(grp, row + d, col), device_id_type=MESH
            )

    for t in tables:
        t.start()
    for h in range(hg):
        for a in range(3):
            own[h][a].start()
    for w in weights:
        w.start()
    for t in tables:
        t.wait()

    lane = lax.broadcasted_iota(jnp.int32, (8, 128), 1)
    sub = lax.broadcasted_iota(jnp.int32, (T, 1), 0)
    code_row = jnp.full((8, 128), -1, jnp.int32)
    owner_col = jnp.zeros((T, 1), jnp.int32)
    live_col = jnp.zeros((T, 1), jnp.int32)
    for t in range(tiles):
        own_t, cnt_t = owner_ref[t], count_ref[t]
        code_row = jnp.where(
            (lane // TILE == t) & (lane % TILE < cnt_t) & (lane < T), own_t, code_row
        )
        owner_col = jnp.where(sub // TILE == t, own_t, owner_col)
        live_col = jnp.where((sub // TILE == t) & (sub % TILE < cnt_t), 1, live_col)
    code[0] = code_row.astype(jnp.float32)

    def near_ok(d):
        return (row - d >= 0) & (row - d < R)

    def goes(d):
        return (row + d >= 0) & (row + d < R)

    for i, d in enumerate(near):
        @pl.when(jnp.logical_not(near_ok(d)))
        def _():
            nb[i + 1] = jnp.zeros((T, LAT), jnp.bfloat16)
            code[i + 1] = jnp.full((8, 128), -1.0, jnp.float32)

    pl.semaphore_wait(
        barrier, len(greeted) + sum([near_ok(d).astype(jnp.int32) for d in near])
    )

    def far(k):
        down = jnp.where(G - 1 - k > g, G - 1 - k, G - 2 - k)
        return jnp.where(2 * g < G, down, jnp.where(k < g, k, k + 1))

    def close(k):
        return far(G - 2 - k)

    def z_copy(h, a, to):
        return pltpu.make_async_remote_copy(
            src_ref=arrays[a][0].at[:, head_cols(to, h)],
            dst_ref=slot(a, h, g),
            send_sem=z_send.at[h, a, to],
            recv_sem=z_recv.at[h, a, g],
            device_id=(grp, to * S + s, col),
            device_id_type=MESH,
        )

    z_copies = {}
    def z_start(kinds):
        for h, a in [(h, a) for a in kinds for h in range(hg)]:
            for k in range(G - 1):
                z_copies[h, a, k] = z_copy(h, a, far(k))
                z_copies[h, a, k].start()

    def z_arrived(h, a, frm):
        pltpu.make_async_remote_copy(
            src_ref=slot(a, h, frm),
            dst_ref=slot(a, h, frm),
            send_sem=z_send.at[h, a, frm],
            recv_sem=z_recv.at[h, a, frm],
            device_id=(grp, frm * S + s, col),
            device_id_type=MESH,
        ).wait_recv()

    z_start((1, 2))

    def m_copy(i, d):
        return pltpu.make_async_remote_copy(
            src_ref=code.at[0],
            dst_ref=code.at[i + 1],
            send_sem=m_send.at[i],
            recv_sem=m_recv.at[i],
            device_id=(grp, row + d, col),
            device_id_type=MESH,
        )

    for i, d in enumerate(near):
        @pl.when(goes(d))
        def _():
            m_copy(i, d).start()

    s_copies, c_copies = {}, {}

    def c_forward(h, a, j):
        buf = arrays[a][1]
        src = lax.rem(s - j + S, S)
        for d in range(1, C):
            c_copies[h, a, j, d] = pltpu.make_async_remote_copy(
                src_ref=buf.at[h, src, col],
                dst_ref=buf.at[h, src, col],
                send_sem=c_send.at[h, a - 1, j, d - 1],
                recv_sem=c_recv.at[h, a - 1, j, d - 1],
                device_id=(grp, row, lax.rem(col + d, C)),
                device_id_type=MESH,
            )
            c_copies[h, a, j, d].start()

    def s_forward(h, a, frm, e):
        buf = arrays[a][1]
        block = buf.at[h, s, col, frm]
        for d in range(1, S):
            s_copies[h, a, e, d] = pltpu.make_async_remote_copy(
                src_ref=block,
                dst_ref=block,
                send_sem=s_send.at[h, a - 1, frm, d - 1],
                recv_sem=s_recv.at[h, a - 1, frm, d - 1],
                device_id=(grp, g * S + lax.rem(s + d, S), col),
                device_id_type=MESH,
            )
            s_copies[h, a, e, d].start()

    def spread(h, kinds=(1, 2)):
        for a in kinds:
            for k in range(G - 1):
                z_arrived(h, a, close(k))
                s_forward(h, a, close(k), k + 1)
            c_forward(h, a, 0)

    def pass_on(h, kinds=(1, 2)):
        for a in kinds:
            for d in range(1, S):
                for e in range(G):
                    s_copies[h, a, e, d].wait_recv()
                c_forward(h, a, d)

    keys = S * C * G * T
    fold = math.log2(math.e) / math.sqrt(HEAD)

    def soften(h):
        query = qb[h].reshape(G * T, HEAD)
        key = kb[h].reshape(keys, HEAD)
        scores = lax.dot_general(
            query, key, (((1,), (1,)), ((), ())), preferred_element_type=jnp.float32
        )
        largest = jnp.max(scores, axis=1, keepdims=True)
        terms = jnp.exp2((scores - largest) * fold)
        return terms.astype(jnp.bfloat16), jnp.sum(terms, axis=1, keepdims=True)

    def blend(h, terms, total):
        value = vb[h].reshape(keys, HEAD)
        mixed = jnp.dot(terms, value, preferred_element_type=jnp.float32)
        return (mixed / total).astype(jnp.bfloat16)

    def c_arrive(h, a):
        for j in range(S):
            for d in range(1, C):
                c_copies[h, a, j, d].wait_recv()

    def ready(h):
        own[h][0].wait()
        for k in range(G - 1):
            z_arrived(h, 0, close(k))
        c_arrive(h, 1)

    for h in range(hg):
        for a in (1, 2):
            own[h][a].wait()
            s_forward(h, a, g, 0)
    for w in weights:
        w.wait()
    for h in range(hg):
        spread(h, (1,))
    for h in range(hg):
        spread(h, (2,))
        if h == 1:
            z_start((0,))
    for h in range(hg):
        pass_on(h, (1,))
    last = hg - 1
    weighed = []
    for h in range(last):
        pass_on(h, (2,))
        if h > 0:
            for e in range(last):
                ready(e)
            weighed = [soften(e) for e in range(last)]
    pass_on(last, (2,))
    for h in range(hg):
        c_arrive(h, 2)
    ready(last)
    weighed.append(soften(last))
    share = jnp.dot(
        jnp.concatenate([blend(h, *weighed[h]) for h in range(hg)], axis=1), wo[...],
        preferred_element_type=jnp.float32,
    ).reshape(G, T, LAT)
    part_out[...] = share.astype(jnp.bfloat16)
    p_copies = {}
    for k in range(G - 1):
        to = far(k)
        p_copies[k] = pltpu.make_async_remote_copy(
            src_ref=part_out.at[to],
            dst_ref=part_in.at[g],
            send_sem=p_send.at[to],
            recv_sem=p_recv.at[g],
            device_id=(grp, to * S + s, col),
            device_id_type=MESH,
        )
        p_copies[k].start()
    acc[...] = share
    velocity = acc[g]
    for i, d in enumerate(near):
        @pl.when(near_ok(d))
        def _():
            m_copy(i, d).wait_recv()
    codes = jnp.concatenate([code[i, 0:1, 0:T] for i in range(n_near + 1)], axis=1)
    spots = jnp.concatenate(
        [
            ((row - d) * C + col) * T + lax.broadcasted_iota(jnp.int32, (1, T), 1)
            for d in [0] + near
        ],
        axis=1,
    )
    mine = (row * C + col) * T + sub
    same = codes == owner_col.astype(jnp.float32)
    gap_f = jnp.abs(mine // (GH * GW) - spots // (GH * GW))
    gap_h = jnp.abs(mine // GW % GH - spots // GW % GH)
    gap_w = jnp.abs(mine % GW - spots % GW)
    for j in range(RHEADS):
        ok = (
            same
            & (gap_f <= reach_ref[j, 0])
            & (gap_h <= reach_ref[j, 1])
            & (gap_w <= reach_ref[j, 2])
        )
        bias[j * T : (j + 1) * T] = jnp.where(ok, 0.0, NEG)
    for k in range(G - 1):
        frm = close(k)
        pltpu.make_async_remote_copy(
            src_ref=part_in.at[frm],
            dst_ref=part_in.at[frm],
            send_sem=p_send.at[frm],
            recv_sem=p_recv.at[frm],
            device_id=(grp, frm * S + s, col),
            device_id_type=MESH,
        ).wait_recv()
        velocity = velocity + part_in[frm].astype(jnp.float32)
    updated = lat[...] + 0.5 * velocity
    fine = updated.astype(jnp.bfloat16)
    nb[0] = fine

    def n_copy(i, d):
        return pltpu.make_async_remote_copy(
            src_ref=nb.at[0],
            dst_ref=nb.at[i + 1],
            send_sem=n_send.at[i],
            recv_sem=n_recv.at[i],
            device_id=(grp, row + d, col),
            device_id_type=MESH,
        )

    for i, d in enumerate(near):
        @pl.when(goes(d))
        def _():
            n_copy(i, d).start()
    upd_ref[...] = 0.5 * velocity
    rquery = jnp.dot(fine, rw[0], preferred_element_type=jnp.float32).astype(jnp.bfloat16)
    rhead = LAT // RHEADS
    part_of = lax.broadcasted_iota(jnp.int32, (T, LAT), 1) // rhead
    stacked = jnp.concatenate(
        [jnp.where(part_of == j, rquery, jnp.zeros_like(rquery)) for j in range(RHEADS)], axis=0
    )
    for i, d in enumerate(near):
        @pl.when(near_ok(d))
        def _():
            n_copy(i, d).wait_recv()
    around = nb[...].reshape((n_near + 1) * T, LAT)
    rkey = jnp.dot(around, rw[1], preferred_element_type=jnp.float32).astype(jnp.bfloat16)
    rvalue = jnp.dot(around, rw[2], preferred_element_type=jnp.float32).astype(jnp.bfloat16)
    scores = lax.dot_general(
        stacked, rkey, (((1,), (1,)), ((), ())), preferred_element_type=jnp.float32
    )
    scores = scores * (1.0 / math.sqrt(rhead)) + bias[...]
    terms = jnp.exp(scores - jnp.max(scores, axis=1, keepdims=True))
    total = jnp.sum(terms, axis=1, keepdims=True)
    mixed = jnp.dot(terms.astype(jnp.bfloat16), rvalue, preferred_element_type=jnp.float32) / total
    joined = mixed[0:T]
    for j in range(1, RHEADS):
        joined = jnp.where(part_of == j, mixed[j * T : (j + 1) * T], joined)
    delta = jnp.dot(
        joined.astype(jnp.bfloat16), ro[...], preferred_element_type=jnp.float32
    ).astype(jnp.bfloat16)
    ref_ref[...] = jnp.where(live_col > 0, delta.astype(jnp.float32), 0.0)

    for copies in (z_copies, s_copies, c_copies, p_copies):
        for copy in copies.values():
            copy.wait_send()
    for i, d in enumerate(near):
        @pl.when(goes(d))
        def _():
            m_copy(i, d).wait_send()
            n_copy(i, d).wait_send()


def per_device(
    queries, key_rows, value_rows, latent, out_proj, tile_owner, tile_count, window_reach,
    refine_query, refine_key, refine_value, refine_out,
):
    R, C = lax.axis_size("row"), lax.axis_size("col")
    T = queries.shape[0]
    heads = queries.shape[1] // HEAD
    G = math.gcd(heads, R)
    S = R // G
    hg = heads // G
    near = near_rows(R, C, T)
    n = len(near)
    any_spec = pl.BlockSpec(memory_space=pl.ANY)
    vmem = pl.BlockSpec(memory_space=pltpu.VMEM)
    dma = pltpu.SemaphoreType.DMA
    bf16, f32 = jnp.bfloat16, jnp.float32
    half, delta = pl.pallas_call(
        functools.partial(kernel, (G, S, C, hg, T), near),
        out_shape=(
            pltpu.VMEM((T, LAT), f32),
            pltpu.VMEM((T, LAT), f32),
        ),
        in_specs=[any_spec] * 12,
        out_specs=(vmem, vmem),
        scratch_shapes=[
            pltpu.VMEM((hg, G, T, HEAD), bf16),
            pltpu.VMEM((hg, S, C, G, T, HEAD), bf16),
            pltpu.VMEM((hg, S, C, G, T, HEAD), bf16),
            pltpu.VMEM((hg * HEAD, LAT), bf16),
            pltpu.VMEM((T, LAT), f32),
            pltpu.VMEM((3, LAT, LAT), bf16),
            pltpu.VMEM((LAT, LAT), bf16),
            pltpu.VMEM((G, T, LAT), f32),
            pltpu.VMEM((G, T, LAT), bf16),
            pltpu.VMEM((G, T, LAT), bf16),
            pltpu.VMEM((n + 1, T, LAT), bf16),
            pltpu.VMEM((n + 1, 8, 128), f32),
            pltpu.VMEM((RHEADS * T, (n + 1) * T), f32),
            pltpu.SMEM((T // TILE,), jnp.int32),
            pltpu.SMEM((T // TILE,), jnp.int32),
            pltpu.SMEM((RHEADS, 3), jnp.int32),
            dma((hg, 3, G)),
            dma((hg, 3, G)),
            dma((hg, 2, G, max(S - 1, 1))),
            dma((hg, 2, G, max(S - 1, 1))),
            dma((hg, 2, S, max(C - 1, 1))),
            dma((hg, 2, S, max(C - 1, 1))),
            dma((G,)),
            dma((G,)),
            dma((n,)),
            dma((n,)),
            dma((n,)),
            dma((n,)),
            dma((hg, 3)),
            dma((6,)),
            dma((3,)),
        ],
        compiler_params=pltpu.CompilerParams(collective_id=0, has_side_effects=True),
    )(
        queries, key_rows, value_rows, latent, out_proj, tile_owner.reshape(-1), tile_count,
        window_reach, refine_query, refine_key, refine_value, refine_out,
    )
    updated = latent + half
    return updated, updated + delta


def solution(mesh):
    return jax.shard_map(
        per_device,
        mesh=mesh,
        in_specs=(
            P(("grp", "row", "col"), None),
            P(("grp", "row", "col"), None),
            P(("grp", "row", "col"), None),
            P(("grp", "row", "col"), None),
            P(),
            P(("grp", "row", "col"), None),
            P(("grp", "row", "col")),
            P(),
            P(),
            P(),
            P(),
            P(),
        ),
        out_specs=(P(("grp", "row", "col"), None), P(("grp", "row", "col"), None)),
        check_vma=False,
    )
```

```python
import functools
import math

import jax
import jax.numpy as jnp
import numpy as np
from jax import lax
from jax.experimental import pallas as pl
from jax.experimental.pallas import tpu as pltpu
from jax.sharding import PartitionSpec as P

HEAD = 128
LAT = 128
RHEADS = 2
TILE = 4
GW = 64
GH = 64
MAX_REACH = 3
MESH = pl.DeviceIdType.MESH
NEG = -1e30


def near_rows(rows, cols, tok):
    spots = {}
    for r in range(rows):
        for c in range(cols):
            p = (r * cols + c) * tok + np.arange(tok)
            spots[r, c] = np.unique(np.stack([p // (GH * GW), p // GW % GH], 1), axis=0)
    found = []
    for d in sorted(range(1 - rows, rows), key=abs):
        if d == 0:
            continue
        hit = False
        for r in range(max(0, -d), min(rows, rows - d)):
            for c in range(cols):
                gap = np.abs(spots[r, c][:, None] - spots[r + d, c][None])
                hit = hit or bool((gap.max(-1) <= MAX_REACH).any())
        if hit:
            found.append(d)
    return found


def kernel(
    dims, near,
    q_hbm, k_hbm, v_hbm, lat_hbm, wo_hbm, owner_hbm, count_hbm, reach_hbm,
    rq_hbm, rk_hbm, rv_hbm, ro_hbm,
    upd_ref, ref_ref,
    qb, kb, vb, wo, lat, rw, ro, fused, acc, part_out, part_in, nb, code, bias,
    owner_ref, count_ref, reach_ref,
    z_send, z_recv, s_send, s_recv, c_send, c_recv, p_send, p_recv,
    n_send, n_recv, m_send, m_recv, own_sem, w_sem, i_sem,
):
    G, S, C, hg, T = dims
    R = G * S
    grp = lax.axis_index("grp")
    row = lax.axis_index("row")
    col = lax.axis_index("col")
    g = row // S
    s = row % S
    n_near = len(near)
    tiles = T // TILE

    def head_cols(group, h):
        return pl.ds(pl.multiple_of((group * hg + h) * HEAD, HEAD), HEAD)

    arrays = ((q_hbm, qb), (k_hbm, kb), (v_hbm, vb))

    def slot(a, h, group):
        return qb.at[h, group] if a == 0 else arrays[a][1].at[h, s, col, group]

    own = [
        [
            pltpu.make_async_copy(
                arrays[a][0].at[:, head_cols(g, h)], slot(a, h, g), own_sem.at[h, a]
            )
            for a in range(3)
        ]
        for h in range(hg)
    ]
    depth = hg * HEAD
    weights = [
        pltpu.make_async_copy(
            wo_hbm.at[pl.ds(pl.multiple_of(g * depth, depth), depth)], wo, w_sem.at[0]
        ),
        pltpu.make_async_copy(lat_hbm, lat, w_sem.at[1]),
        pltpu.make_async_copy(rq_hbm, rw.at[0], w_sem.at[2]),
        pltpu.make_async_copy(rk_hbm, rw.at[1], w_sem.at[3]),
        pltpu.make_async_copy(rv_hbm, rw.at[2], w_sem.at[4]),
        pltpu.make_async_copy(ro_hbm, ro, w_sem.at[5]),
    ]

    tables = [
        pltpu.make_async_copy(owner_hbm, owner_ref, i_sem.at[0]),
        pltpu.make_async_copy(count_hbm, count_ref, i_sem.at[1]),
        pltpu.make_async_copy(reach_hbm, reach_ref, i_sem.at[2]),
    ]

    barrier = pltpu.get_barrier_semaphore()
    greeted = (
        [(lax.rem(g + d, G) * S + s, col) for d in range(1, G)]
        + [(g * S + lax.rem(s + d, S), col) for d in range(1, S)]
        + [(row, lax.rem(col + d, C)) for d in range(1, C)]
    )
    for r2, c2 in greeted:
        pl.semaphore_signal(barrier, inc=1, device_id=(grp, r2, c2), device_id_type=MESH)

    for d in near:
        @pl.when((row + d >= 0) & (row + d < R))
        def _():
            pl.semaphore_signal(
                barrier, inc=1, device_id=(grp, row + d, col), device_id_type=MESH
            )

    for t in tables:
        t.start()
    for h in range(hg):
        for a in range(3):
            own[h][a].start()
    for w in weights:
        w.start()
    for t in tables:
        t.wait()

    lane = lax.broadcasted_iota(jnp.int32, (8, 128), 1)
    sub = lax.broadcasted_iota(jnp.int32, (T, 1), 0)
    code_row = jnp.full((8, 128), -1, jnp.int32)
    owner_col = jnp.zeros((T, 1), jnp.int32)
    live_col = jnp.zeros((T, 1), jnp.int32)
    for t in range(tiles):
        own_t, cnt_t = owner_ref[t], count_ref[t]
        code_row = jnp.where(
            (lane // TILE == t) & (lane % TILE < cnt_t) & (lane < T), own_t, code_row
        )
        owner_col = jnp.where(sub // TILE == t, own_t, owner_col)
        live_col = jnp.where((sub // TILE == t) & (sub % TILE < cnt_t), 1, live_col)
    code[0] = code_row.astype(jnp.float32)

    def near_ok(d):
        return (row - d >= 0) & (row - d < R)

    def goes(d):
        return (row + d >= 0) & (row + d < R)

    for i, d in enumerate(near):
        @pl.when(jnp.logical_not(near_ok(d)))
        def _():
            nb[i + 1] = jnp.zeros((T, LAT), jnp.bfloat16)
            code[i + 1] = jnp.full((8, 128), -1.0, jnp.float32)

    pl.semaphore_wait(
        barrier, len(greeted) + sum([near_ok(d).astype(jnp.int32) for d in near])
    )

    def far(k):
        down = jnp.where(G - 1 - k > g, G - 1 - k, G - 2 - k)
        return jnp.where(2 * g < G, down, jnp.where(k < g, k, k + 1))

    def close(k):
        return far(G - 2 - k)

    def z_copy(h, a, to):
        return pltpu.make_async_remote_copy(
            src_ref=arrays[a][0].at[:, head_cols(to, h)],
            dst_ref=slot(a, h, g),
            send_sem=z_send.at[h, a, to],
            recv_sem=z_recv.at[h, a, g],
            device_id=(grp, to * S + s, col),
            device_id_type=MESH,
        )

    z_copies = {}
    def z_start(kinds):
        for h, a in [(h, a) for a in kinds for h in range(hg)]:
            for k in range(G - 1):
                z_copies[h, a, k] = z_copy(h, a, far(k))
                z_copies[h, a, k].start()

    def z_arrived(h, a, frm):
        pltpu.make_async_remote_copy(
            src_ref=slot(a, h, frm),
            dst_ref=slot(a, h, frm),
            send_sem=z_send.at[h, a, frm],
            recv_sem=z_recv.at[h, a, frm],
            device_id=(grp, frm * S + s, col),
            device_id_type=MESH,
        ).wait_recv()

    z_start((1, 2))

    def m_copy(i, d):
        return pltpu.make_async_remote_copy(
            src_ref=code.at[0],
            dst_ref=code.at[i + 1],
            send_sem=m_send.at[i],
            recv_sem=m_recv.at[i],
            device_id=(grp, row + d, col),
            device_id_type=MESH,
        )

    for i, d in enumerate(near):
        @pl.when(goes(d))
        def _():
            m_copy(i, d).start()

    s_copies, c_copies = {}, {}

    def c_forward(h, a, j):
        buf = arrays[a][1]
        src = lax.rem(s - j + S, S)
        for d in range(1, C):
            c_copies[h, a, j, d] = pltpu.make_async_remote_copy(
                src_ref=buf.at[h, src, col],
                dst_ref=buf.at[h, src, col],
                send_sem=c_send.at[h, a - 1, j, d - 1],
                recv_sem=c_recv.at[h, a - 1, j, d - 1],
                device_id=(grp, row, lax.rem(col + d, C)),
                device_id_type=MESH,
            )
            c_copies[h, a, j, d].start()

    def s_forward(h, a, frm, e):
        buf = arrays[a][1]
        block = buf.at[h, s, col, frm]
        for d in range(1, S):
            s_copies[h, a, e, d] = pltpu.make_async_remote_copy(
                src_ref=block,
                dst_ref=block,
                send_sem=s_send.at[h, a - 1, frm, d - 1],
                recv_sem=s_recv.at[h, a - 1, frm, d - 1],
                device_id=(grp, g * S + lax.rem(s + d, S), col),
                device_id_type=MESH,
            )
            s_copies[h, a, e, d].start()

    def spread(h, kinds=(1, 2)):
        for a in kinds:
            for k in range(G - 1):
                z_arrived(h, a, close(k))
                s_forward(h, a, close(k), k + 1)
            c_forward(h, a, 0)

    def pass_on(h, kinds=(1, 2)):
        for a in kinds:
            for d in range(1, S):
                for e in range(G):
                    s_copies[h, a, e, d].wait_recv()
                c_forward(h, a, d)

    keys = S * C * G * T
    fold = math.log2(math.e) / math.sqrt(HEAD)

    def soften(h):
        query = qb[h].reshape(G * T, HEAD)
        key = kb[h].reshape(keys, HEAD)
        scores = lax.dot_general(
            query, key, (((1,), (1,)), ((), ())), preferred_element_type=jnp.float32
        )
        largest = jnp.max(scores, axis=1, keepdims=True)
        terms = jnp.exp2((scores - largest) * fold)
        return terms.astype(jnp.bfloat16), jnp.sum(terms, axis=1, keepdims=True)

    def blend(h, terms, total):
        value = vb[h].reshape(keys, HEAD)
        mixed = jnp.dot(terms, value, preferred_element_type=jnp.float32)
        return (mixed / total).astype(jnp.bfloat16)

    def c_arrive(h, a):
        for j in range(S):
            for d in range(1, C):
                c_copies[h, a, j, d].wait_recv()

    def ready(h):
        own[h][0].wait()
        for k in range(G - 1):
            z_arrived(h, 0, close(k))
        c_arrive(h, 1)

    for h in range(hg):
        for a in (1, 2):
            own[h][a].wait()
            s_forward(h, a, g, 0)
    for w in weights:
        w.wait()
    rhead = LAT // RHEADS
    part_of = lax.broadcasted_iota(jnp.int32, (T, LAT), 1) // rhead
    column_of = lax.broadcasted_iota(jnp.int32, (LAT, LAT), 1) // rhead
    for j in range(RHEADS):
        value_part = jnp.where(column_of == j, rw[2], jnp.zeros_like(rw[2]))
        fused[j * LAT : (j + 1) * LAT] = jnp.dot(
            value_part, ro[...], preferred_element_type=jnp.float32
        ).astype(jnp.bfloat16)
    for h in range(hg):
        spread(h, (1,))
    for h in range(hg):
        spread(h, (2,))
        if h == 1:
            z_start((0,))
    for h in range(hg):
        pass_on(h, (1,))
    last = hg - 1
    weighed = []
    for h in range(last):
        pass_on(h, (2,))
        if h > 0:
            for e in range(last):
                ready(e)
            weighed = [soften(e) for e in range(last)]
    pass_on(last, (2,))
    for h in range(hg):
        c_arrive(h, 2)
    ready(last)
    weighed.append(soften(last))
    share = jnp.dot(
        jnp.concatenate([blend(h, *weighed[h]) for h in range(hg)], axis=1), wo[...],
        preferred_element_type=jnp.float32,
    ).reshape(G, T, LAT)
    part_out[...] = share.astype(jnp.bfloat16)
    p_copies = {}
    for k in range(G - 1):
        to = far(k)
        p_copies[k] = pltpu.make_async_remote_copy(
            src_ref=part_out.at[to],
            dst_ref=part_in.at[g],
            send_sem=p_send.at[to],
            recv_sem=p_recv.at[g],
            device_id=(grp, to * S + s, col),
            device_id_type=MESH,
        )
        p_copies[k].start()
    acc[...] = share
    velocity = acc[g]
    for i, d in enumerate(near):
        @pl.when(near_ok(d))
        def _():
            m_copy(i, d).wait_recv()
    codes = jnp.concatenate([code[i, 0:1, 0:T] for i in range(n_near + 1)], axis=1)
    spots = jnp.concatenate(
        [
            ((row - d) * C + col) * T + lax.broadcasted_iota(jnp.int32, (1, T), 1)
            for d in [0] + near
        ],
        axis=1,
    )
    mine = (row * C + col) * T + sub
    same = codes == owner_col.astype(jnp.float32)
    gap_f = jnp.abs(mine // (GH * GW) - spots // (GH * GW))
    gap_h = jnp.abs(mine // GW % GH - spots // GW % GH)
    gap_w = jnp.abs(mine % GW - spots % GW)
    for j in range(RHEADS):
        ok = (
            same
            & (gap_f <= reach_ref[j, 0])
            & (gap_h <= reach_ref[j, 1])
            & (gap_w <= reach_ref[j, 2])
        )
        bias[j * T : (j + 1) * T] = jnp.where(ok, 0.0, NEG)
    for k in range(G - 1):
        frm = close(k)
        pltpu.make_async_remote_copy(
            src_ref=part_in.at[frm],
            dst_ref=part_in.at[frm],
            send_sem=p_send.at[frm],
            recv_sem=p_recv.at[frm],
            device_id=(grp, frm * S + s, col),
            device_id_type=MESH,
        ).wait_recv()
        velocity = velocity + part_in[frm].astype(jnp.float32)
    updated = lat[...] + 0.5 * velocity
    fine = updated.astype(jnp.bfloat16)
    nb[0] = fine

    def n_copy(i, d):
        return pltpu.make_async_remote_copy(
            src_ref=nb.at[0],
            dst_ref=nb.at[i + 1],
            send_sem=n_send.at[i],
            recv_sem=n_recv.at[i],
            device_id=(grp, row + d, col),
            device_id_type=MESH,
        )

    for i, d in enumerate(near):
        @pl.when(goes(d))
        def _():
            n_copy(i, d).start()
    upd_ref[...] = 0.5 * velocity
    rquery = jnp.dot(fine, rw[0], preferred_element_type=jnp.float32).astype(jnp.bfloat16)
    stacked = jnp.concatenate(
        [jnp.where(part_of == j, rquery, jnp.zeros_like(rquery)) for j in range(RHEADS)], axis=0
    )
    probe = lax.dot_general(
        stacked, rw[1], (((1,), (1,)), ((), ())), preferred_element_type=jnp.float32
    ).astype(jnp.bfloat16)
    for i, d in enumerate(near):
        @pl.when(near_ok(d))
        def _():
            n_copy(i, d).wait_recv()
    around = nb[...].reshape((n_near + 1) * T, LAT)
    scores = lax.dot_general(
        probe, around, (((1,), (1,)), ((), ())), preferred_element_type=jnp.float32
    )
    scores = scores * (1.0 / math.sqrt(rhead)) + bias[...]
    terms = jnp.exp(scores - jnp.max(scores, axis=1, keepdims=True))
    total = jnp.sum(terms, axis=1, keepdims=True)
    mixed = jnp.dot(terms.astype(jnp.bfloat16), around, preferred_element_type=jnp.float32)
    mixed = (mixed / total).astype(jnp.bfloat16)
    joined = jnp.concatenate([mixed[j * T : (j + 1) * T] for j in range(RHEADS)], axis=1)
    delta = jnp.dot(joined, fused[...], preferred_element_type=jnp.float32).astype(jnp.bfloat16)
    ref_ref[...] = jnp.where(live_col > 0, delta.astype(jnp.float32), 0.0)

    for copies in (z_copies, s_copies, c_copies, p_copies):
        for copy in copies.values():
            copy.wait_send()
    for i, d in enumerate(near):
        @pl.when(goes(d))
        def _():
            m_copy(i, d).wait_send()
            n_copy(i, d).wait_send()


def per_device(
    queries, key_rows, value_rows, latent, out_proj, tile_owner, tile_count, window_reach,
    refine_query, refine_key, refine_value, refine_out,
):
    R, C = lax.axis_size("row"), lax.axis_size("col")
    T = queries.shape[0]
    heads = queries.shape[1] // HEAD
    G = math.gcd(heads, R)
    S = R // G
    hg = heads // G
    near = near_rows(R, C, T)
    n = len(near)
    any_spec = pl.BlockSpec(memory_space=pl.ANY)
    vmem = pl.BlockSpec(memory_space=pltpu.VMEM)
    dma = pltpu.SemaphoreType.DMA
    bf16, f32 = jnp.bfloat16, jnp.float32
    half, delta = pl.pallas_call(
        functools.partial(kernel, (G, S, C, hg, T), near),
        out_shape=(
            pltpu.VMEM((T, LAT), f32),
            pltpu.VMEM((T, LAT), f32),
        ),
        in_specs=[any_spec] * 12,
        out_specs=(vmem, vmem),
        scratch_shapes=[
            pltpu.VMEM((hg, G, T, HEAD), bf16),
            pltpu.VMEM((hg, S, C, G, T, HEAD), bf16),
            pltpu.VMEM((hg, S, C, G, T, HEAD), bf16),
            pltpu.VMEM((hg * HEAD, LAT), bf16),
            pltpu.VMEM((T, LAT), f32),
            pltpu.VMEM((3, LAT, LAT), bf16),
            pltpu.VMEM((LAT, LAT), bf16),
            pltpu.VMEM((RHEADS * LAT, LAT), bf16),
            pltpu.VMEM((G, T, LAT), f32),
            pltpu.VMEM((G, T, LAT), bf16),
            pltpu.VMEM((G, T, LAT), bf16),
            pltpu.VMEM((n + 1, T, LAT), bf16),
            pltpu.VMEM((n + 1, 8, 128), f32),
            pltpu.VMEM((RHEADS * T, (n + 1) * T), f32),
            pltpu.SMEM((T // TILE,), jnp.int32),
            pltpu.SMEM((T // TILE,), jnp.int32),
            pltpu.SMEM((RHEADS, 3), jnp.int32),
            dma((hg, 3, G)),
            dma((hg, 3, G)),
            dma((hg, 2, G, max(S - 1, 1))),
            dma((hg, 2, G, max(S - 1, 1))),
            dma((hg, 2, S, max(C - 1, 1))),
            dma((hg, 2, S, max(C - 1, 1))),
            dma((G,)),
            dma((G,)),
            dma((n,)),
            dma((n,)),
            dma((n,)),
            dma((n,)),
            dma((hg, 3)),
            dma((6,)),
            dma((3,)),
        ],
        compiler_params=pltpu.CompilerParams(collective_id=0, has_side_effects=True),
    )(
        queries, key_rows, value_rows, latent, out_proj, tile_owner.reshape(-1), tile_count,
        window_reach, refine_query, refine_key, refine_value, refine_out,
    )
    updated = latent + half
    return updated, updated + delta


def solution(mesh):
    return jax.shard_map(
        per_device,
        mesh=mesh,
        in_specs=(
            P(("grp", "row", "col"), None),
            P(("grp", "row", "col"), None),
            P(("grp", "row", "col"), None),
            P(("grp", "row", "col"), None),
            P(),
            P(("grp", "row", "col"), None),
            P(("grp", "row", "col")),
            P(),
            P(),
            P(),
            P(),
            P(),
        ),
        out_specs=(P(("grp", "row", "col"), None), P(("grp", "row", "col"), None)),
        check_vma=False,
    )
```
